32 devices in a mesh: section: 4 (over z), seq: 8 (over y, x, core).
Axes of the slice: x: 2, y: 2, z: 4, core: 2. Of those that a mesh axis runs over, the one named last changes fastest.
Arguments:
- query_projection: bfloat16 [4, 2048, 4096], P('section', 'seq'), may hold values from -6 to 6
- k_proj: bfloat16 [4, 2048, 512], P('section', 'seq'), may hold values from -6 to 6
- value_projection: bfloat16 [4, 2048, 512], P('section', 'seq'), may hold values from -6 to 6
- doc_lengths: int32 [4, 8], P('section'), may hold values from 1 to 512, 2048 in all within a row
Outputs:
- next_rows: bfloat16 [4, 2048, 4096], P('section', 'seq')
The draws below stay inside these ranges and needn't reach their ends.
Inputs may be any that keep to these rules, and one draw needn't show every extreme that they name: `doc_lengths`: in each section the largest length is exactly 512.
All inputs are finite; a program needn't handle non-finite values.
Results may differ from the reference program's by a relative error of at most 0.0037.
Values may be sent and summed in bfloat16 or wider, within the bound.
A program may use at most 64 MiB of HBM per device.

```python
import math
import jax
import jax.numpy as jnp
import numpy as np
from jax import lax

QUERY_HEADS = 32
KEY_VALUE_HEADS = 4
HEAD_SIZE = 128
SHARD_TOKENS = 256
CASCADE_PARTS = 4
PACKED_LENGTH = 2048
NDOCS = 8
DOC_MAX = 512
N_SEQ = 8


def paired_draw(key):
    base = jax.random.fold_in(key, 11)
    query_seed, random_key_seed = jax.random.split(base, 2)
    head_groups = QUERY_HEADS // KEY_VALUE_HEADS
    query_matrix = jnp.clip(jax.random.normal(query_seed, (CASCADE_PARTS, PACKED_LENGTH, KEY_VALUE_HEADS, head_groups, HEAD_SIZE), jnp.float32), -6.0, 6.0)
    key_matrix = jnp.clip(jax.random.normal(random_key_seed, (CASCADE_PARTS, PACKED_LENGTH, KEY_VALUE_HEADS, HEAD_SIZE), jnp.float32), -6.0, 6.0)
    return (query_matrix.reshape(CASCADE_PARTS, PACKED_LENGTH, QUERY_HEADS * HEAD_SIZE), key_matrix.reshape(CASCADE_PARTS, PACKED_LENGTH, KEY_VALUE_HEADS * HEAD_SIZE))


def draw_query_projection(key, part):
    return paired_draw(key)[0].astype(jnp.bfloat16)


def draw_k_proj(key, part):
    return paired_draw(key)[1].astype(jnp.bfloat16)


def block_levels(own_key, dims, cuts, least, largest):
    gain = 1.0
    for position, shards_of in cuts:
        steps = jax.random.uniform(jax.random.fold_in(jax.random.fold_in(own_key, 6), position), (shards_of,), jnp.float32, least / len(cuts), largest / len(cuts))
        gain = gain * jnp.repeat(jnp.exp(steps), dims[position] // shards_of).reshape((-1,) + (1,) * (len(dims) - 1 - position))
    return gain


def profile(number_of, total, bound, slope):
    weights = [(1 << 20) // math.isqrt(standing ** slope) + 1 for standing in range(2, number_of + 1)]
    spare, holding = total - bound - (number_of - 1), [1] * (number_of - 1)
    while spare > 0:
        free = [i for i in range(number_of - 1) if holding[i] < bound]
        mass, budget = sum([weights[i] for i in free]), spare
        for i in free:
            addition = min(bound - holding[i], max(1, budget * weights[i] // mass), spare)
            holding[i] = holding[i] + addition
            spare = spare - addition
    return np.array([bound] + holding)


def uneven_parts(key, amount, total, limit, lean):
    if amount == 2:
        one = jax.random.randint(key, (), max(1, total - limit), min(limit, total - 1) + 1)
        return jnp.stack([one, total - one])
    sizes = jnp.asarray(profile(amount, total, limit, lean), jnp.int32)
    couples = (amount - 1) // 2
    source_of, receiver = sizes[1:1 + 2 * couples:2], sizes[2:2 + 2 * couples:2]
    slack = jnp.minimum(source_of - 1, limit - receiver)
    moved = jax.random.randint(jax.random.fold_in(key, 1), (couples,), 0, 1 << 20) % (slack + 1)
    sizes = sizes.at[1:1 + 2 * couples:2].set(source_of - moved).at[2:2 + 2 * couples:2].set(receiver + moved)
    return sizes[jax.random.permutation(jax.random.fold_in(key, 2), amount)]


def bell_draw(rng, dims, width, most, shards=(), held_as=jnp.bfloat16):
    values = width * jax.random.normal(rng, dims, jnp.float32)
    if shards:
        values = values * block_levels(rng, dims, shards, -0.22, 0.18)
    return jnp.clip(values, -most, most).astype(held_as)


def setup_inputs(seed: int = 0) -> dict:
    splits = jax.random.split(jax.random.key(seed), 5)
    query_projection = draw_query_projection(jax.random.fold_in(splits[4], 71), 0)
    k_proj = draw_k_proj(jax.random.fold_in(splits[4], 71), 0)
    value_projection = bell_draw(splits[2], (CASCADE_PARTS, PACKED_LENGTH, KEY_VALUE_HEADS * HEAD_SIZE), 1.0, 6.0, ((0, 4), (1, 8)))
    doc_lengths = jax.vmap(lambda own: uneven_parts(own, NDOCS, PACKED_LENGTH, DOC_MAX, 2))(jax.random.split(splits[3], CASCADE_PARTS)).reshape((CASCADE_PARTS, NDOCS)).astype(jnp.int32)
    return dict(query_projection=query_projection, k_proj=k_proj, value_projection=value_projection, doc_lengths=doc_lengths)


def section_attention(inputs):
    query_matrix, key_matrix, value_matrix, lengths = inputs
    head_groups = QUERY_HEADS // KEY_VALUE_HEADS
    score_scale = 1.0 / (HEAD_SIZE ** 0.5)
    doc_ends = jnp.cumsum(lengths).astype(jnp.int32)
    positions = jnp.arange(PACKED_LENGTH, dtype=jnp.int32)
    doc_starts = jnp.max(jnp.where(doc_ends[None, :] <= positions[:, None], doc_ends[None, :], 0), axis=1).astype(jnp.int32)
    border_width = 2 * SHARD_TOKENS
    extended_keys = jnp.concatenate([jnp.zeros((border_width, KEY_VALUE_HEADS * HEAD_SIZE), key_matrix.dtype), key_matrix], 0)
    extended_values = jnp.concatenate([jnp.zeros((border_width, KEY_VALUE_HEADS * HEAD_SIZE), value_matrix.dtype), value_matrix], 0)

    def block(index):
        leading = (index * SHARD_TOKENS).astype(jnp.int32)
        query_row_block = lax.dynamic_slice_in_dim(query_matrix, leading, SHARD_TOKENS, 0).astype(jnp.float32).reshape(SHARD_TOKENS, KEY_VALUE_HEADS, head_groups, HEAD_SIZE)
        key_row_block = lax.dynamic_slice_in_dim(extended_keys, leading, 3 * SHARD_TOKENS, 0).astype(jnp.float32).reshape(3 * SHARD_TOKENS, KEY_VALUE_HEADS, HEAD_SIZE)
        value_row_block = lax.dynamic_slice_in_dim(extended_values, leading, 3 * SHARD_TOKENS, 0).astype(jnp.float32).reshape(3 * SHARD_TOKENS, KEY_VALUE_HEADS, HEAD_SIZE)
        query_pos = leading + jnp.arange(SHARD_TOKENS, dtype=jnp.int32)
        key_pos = leading - border_width + jnp.arange(3 * SHARD_TOKENS, dtype=jnp.int32)
        starts = lax.dynamic_slice_in_dim(doc_starts, leading, SHARD_TOKENS, 0)
        allowed = (key_pos[None, :] >= starts[:, None]) & (key_pos[None, :] <= query_pos[:, None])
        scores = jnp.einsum('ikgd,jkd->kgij', query_row_block, key_row_block) * score_scale
        scores = jnp.where(allowed[None, None], scores, -jnp.inf)
        row_max = jnp.max(scores, axis=-1, keepdims=True)
        weights = jnp.exp(scores - row_max)
        row_total = jnp.sum(weights, axis=-1)
        rounded = lax.optimization_barrier(weights.astype(jnp.bfloat16)).astype(jnp.float32)
        mixed = jnp.einsum('kgij,jkd->ikgd', rounded, value_row_block)
        mixed = mixed / jnp.transpose(row_total, (2, 0, 1))[..., None]
        return mixed.reshape(SHARD_TOKENS, QUERY_HEADS * HEAD_SIZE).astype(jnp.bfloat16)

    blocks = lax.map(block, jnp.arange(N_SEQ, dtype=jnp.int32))
    return blocks.reshape(PACKED_LENGTH, QUERY_HEADS * HEAD_SIZE)


def reference(query_projection, k_proj, value_projection, doc_lengths):
    attended = lax.map(section_attention, (query_projection, k_proj, value_projection, doc_lengths))
    return jnp.roll(attended, 1, axis=0)
```

```python
import functools
import math

import jax
import jax.numpy as jnp
from jax import lax
from jax.experimental import pallas as pl
from jax.experimental.pallas import tpu as pltpu
from jax.sharding import PartitionSpec as P

QUERY_HEADS = 32
KEY_VALUE_HEADS = 4
HEAD_SIZE = 128
GROUP = QUERY_HEADS // KEY_VALUE_HEADS
MESH = pl.DeviceIdType.MESH
FACTOR = math.log2(math.e) / math.sqrt(HEAD_SIZE)


def kernel(
    n_seq, n_sec, q_ref, k_ref, v_ref, doc_ref, out_ref,
    q_buf, k_buf, v_buf, bias, stage,
    q_sem, own_sem, halo_send, halo_recv, out_send, out_recv,
):
    rows = q_ref.shape[0]
    me = lax.axis_index("seq")
    sec = lax.axis_index("section")
    to_one = lax.rem(me + 1, n_seq)
    to_two = lax.rem(me + 2, n_seq)
    from_one = lax.rem(me + n_seq - 1, n_seq)
    from_two = lax.rem(me + n_seq - 2, n_seq)
    next_sec = lax.rem(sec + 1, n_sec)
    last_sec = lax.rem(sec + n_sec - 1, n_sec)

    barrier = pltpu.get_barrier_semaphore()
    for other in (from_one, from_two, to_one, to_two):
        pl.semaphore_signal(
            barrier, inc=1, device_id={"seq": other}, device_id_type=MESH
        )
    for other in (next_sec, last_sec):
        pl.semaphore_signal(
            barrier, inc=1, device_id={"section": other}, device_id_type=MESH
        )

    def columns(head, count=1):
        return pl.ds(pl.multiple_of(head * HEAD_SIZE, HEAD_SIZE), count * HEAD_SIZE)

    def own_copy(source, buf, group, which):
        return pltpu.make_async_copy(
            source.at[:, columns(group)],
            buf.at[group, pl.ds(2 * rows, rows)],
            own_sem.at[group, which],
        )

    def q_copy(group):
        return pltpu.make_async_copy(
            q_ref.at[:, columns(group * GROUP, GROUP)],
            q_buf.at[:, columns(group * GROUP, GROUP)],
            q_sem.at[group],
        )

    def halo(source, buf, group, which, far):
        return pltpu.make_async_remote_copy(
            src_ref=source.at[:, columns(group)],
            dst_ref=buf.at[group, pl.ds(0 if far else rows, rows)],
            send_sem=halo_send.at[group, which, far],
            recv_sem=halo_recv.at[group, which, far],
            device_id={"seq": to_two if far else to_one},
            device_id_type=MESH,
        )

    def out_copy(head):
        return pltpu.make_async_remote_copy(
            src_ref=stage.at[:, columns(head)],
            dst_ref=out_ref.at[:, columns(head)],
            send_sem=out_send.at[head],
            recv_sem=out_recv.at[head],
            device_id={"section": next_sec},
            device_id_type=MESH,
        )

    pairs = ((k_ref, k_buf), (v_ref, v_buf))
    for group in range(KEY_VALUE_HEADS):
        for which, (source, buf) in enumerate(pairs):
            own_copy(source, buf, group, which).start()
        q_copy(group).start()

    pl.semaphore_wait(barrier, 6)
    for group in range(KEY_VALUE_HEADS):
        for which, (source, buf) in enumerate(pairs):
            for far in (1, 0):
                halo(source, buf, group, which, far).start()

    base = me * rows
    position = base + lax.broadcasted_iota(jnp.int32, (rows, rows), 0)
    column = lax.broadcasted_iota(jnp.int32, (rows, rows), 1)
    start = jnp.zeros((rows, rows), jnp.int32)
    end = jnp.int32(0)
    for doc in range(doc_ref.shape[1]):
        end = end + doc_ref[0, doc]
        start = jnp.where(end <= position, jnp.maximum(start, end), start)
    for place in range(3):
        key = base + (place - 2) * rows + column
        allowed = (key >= start) & (key <= position)
        bias[:, place * rows:(place + 1) * rows] = jnp.where(allowed, 0.0, -jnp.inf)

    for group in range(KEY_VALUE_HEADS):
        q_copy(group).wait()
        for which, (source, buf) in enumerate(pairs):
            own_copy(source, buf, group, which).wait()
            for far in (1, 0):
                halo(source, buf, group, which, far).wait_recv()

        @pl.loop(0, GROUP)
        def _(index):
            head = group * GROUP + index
            query = q_buf[:, columns(head)]
            scores = lax.dot_general(
                query, k_buf[group], (((1,), (1,)), ((), ())),
                preferred_element_type=jnp.float32,
            ) + bias[...]
            most = jnp.max(scores, axis=1, keepdims=True)
            weights = jnp.exp2((scores - most) * FACTOR)
            total = jnp.sum(weights, axis=1, keepdims=True)
            mixed = jnp.dot(
                weights.astype(jnp.bfloat16), v_buf[group],
                preferred_element_type=jnp.float32,
            )
            stage[:, columns(head)] = (mixed / total).astype(jnp.bfloat16)
            out_copy(head).start()

    for group in range(KEY_VALUE_HEADS):
        for which, (source, buf) in enumerate(pairs):
            for far in (1, 0):
                halo(source, buf, group, which, far).wait_send()

    @pl.loop(0, QUERY_HEADS)
    def _(head):
        out_copy(head).wait()


def solution(mesh):
    n_seq, n_sec = mesh.shape["seq"], mesh.shape["section"]

    def local(query_projection, k_proj, value_projection, doc_lengths):
        rows, width = query_projection.shape[1:]
        any_spec = pl.BlockSpec(memory_space=pl.ANY)
        result = pl.pallas_call(
            functools.partial(kernel, n_seq, n_sec),
            out_shape=jax.ShapeDtypeStruct((rows, width), jnp.bfloat16),
            in_specs=[any_spec] * 3 + [pl.BlockSpec(memory_space=pltpu.SMEM)],
            out_specs=any_spec,
            scratch_shapes=[
                pltpu.VMEM((rows, width), jnp.bfloat16),
                pltpu.VMEM((KEY_VALUE_HEADS, 3 * rows, HEAD_SIZE), jnp.bfloat16),
                pltpu.VMEM((KEY_VALUE_HEADS, 3 * rows, HEAD_SIZE), jnp.bfloat16),
                pltpu.VMEM((rows, 3 * rows), jnp.float32),
                pltpu.VMEM((rows, width), jnp.bfloat16),
                pltpu.SemaphoreType.DMA((KEY_VALUE_HEADS,)),
                pltpu.SemaphoreType.DMA((KEY_VALUE_HEADS, 2)),
                pltpu.SemaphoreType.DMA((KEY_VALUE_HEADS, 2, 2)),
                pltpu.SemaphoreType.DMA((KEY_VALUE_HEADS, 2, 2)),
                pltpu.SemaphoreType.DMA((QUERY_HEADS,)),
                pltpu.SemaphoreType.DMA((QUERY_HEADS,)),
            ],
            compiler_params=pltpu.CompilerParams(
                collective_id=0, has_side_effects=True
            ),
        )(query_projection[0], k_proj[0], value_projection[0], doc_lengths)
        return result[None]

    in_specs = (
        P("section", "seq", None),
        P("section", "seq", None),
        P("section", "seq", None),
        P("section", None),
    )
    return jax.shard_map(
        local, mesh=mesh, in_specs=in_specs, out_specs=P("section", "seq", None),
        check_vma=False,
    )
```

```python
import functools
import math

import jax
import jax.numpy as jnp
from jax import lax
from jax.experimental import pallas as pl
from jax.experimental.pallas import tpu as pltpu
from jax.sharding import PartitionSpec as P

QUERY_HEADS = 32
KEY_VALUE_HEADS = 4
HEAD_SIZE = 128
GROUP = QUERY_HEADS // KEY_VALUE_HEADS
RAW = 4
MESH = pl.DeviceIdType.MESH
FACTOR = math.log2(math.e) / math.sqrt(HEAD_SIZE)


def kernel(
    n_seq, n_sec, q_ref, k_ref, v_ref, doc_ref, out_ref,
    q_buf, k_buf, v_buf, bias, stage, doc_own, doc_last, raw_q, raw_k, raw_v,
    q_sem, own_sem, halo_send, halo_recv, out_send, out_recv,
    doc_sem, raw_send, raw_recv, relay_send, relay_recv,
):
    rows = q_ref.shape[0]
    me = lax.axis_index("seq")
    sec = lax.axis_index("section")
    to_one = lax.rem(me + 1, n_seq)
    to_two = lax.rem(me + 2, n_seq)
    from_one = lax.rem(me + n_seq - 1, n_seq)
    from_two = lax.rem(me + n_seq - 2, n_seq)
    next_sec = lax.rem(sec + 1, n_sec)
    last_sec = lax.rem(sec + n_sec - 1, n_sec)

    barrier = pltpu.get_barrier_semaphore()
    for other in (from_one, from_two, to_one, to_two):
        pl.semaphore_signal(
            barrier, inc=1, device_id={"seq": other}, device_id_type=MESH
        )
    for other in (next_sec, last_sec):
        pl.semaphore_signal(
            barrier, inc=1, device_id={"section": other}, device_id_type=MESH
        )

    def columns(head, count=1):
        return pl.ds(pl.multiple_of(head * HEAD_SIZE, HEAD_SIZE), count * HEAD_SIZE)

    def own_copy(source, buf, group, which):
        return pltpu.make_async_copy(
            source.at[:, columns(group)],
            buf.at[group, pl.ds(2 * rows, rows)],
            own_sem.at[group, which],
        )

    def q_copy(group):
        return pltpu.make_async_copy(
            q_ref.at[:, columns(group * GROUP, GROUP)],
            q_buf.at[:, columns(group * GROUP, GROUP)],
            q_sem.at[group],
        )

    def halo(source, buf, group, which, far):
        return pltpu.make_async_remote_copy(
            src_ref=source.at[:, columns(group)],
            dst_ref=buf.at[group, pl.ds(0 if far else rows, rows)],
            send_sem=halo_send.at[group, which, far],
            recv_sem=halo_recv.at[group, which, far],
            device_id={"seq": to_two if far else to_one},
            device_id_type=MESH,
        )

    def out_copy(head):
        return pltpu.make_async_remote_copy(
            src_ref=stage.at[:, columns(head)],
            dst_ref=out_ref.at[:, columns(head)],
            send_sem=out_send.at[head],
            recv_sem=out_recv.at[head],
            device_id={"section": next_sec},
            device_id_type=MESH,
        )

    def raw_copy(source, buf, which):
        return pltpu.make_async_remote_copy(
            src_ref=source,
            dst_ref=buf,
            send_sem=raw_send.at[which],
            recv_sem=raw_recv.at[which],
            device_id={"section": next_sec},
            device_id_type=MESH,
        )

    def relay(buf, which, far):
        return pltpu.make_async_remote_copy(
            src_ref=buf.at[pl.ds(2 * rows, rows)],
            dst_ref=buf.at[pl.ds(0 if far else rows, rows)],
            send_sem=relay_send.at[which, far],
            recv_sem=relay_recv.at[which, far],
            device_id={"seq": to_two if far else to_one},
            device_id_type=MESH,
        )

    raw_columns = pl.ds(0, RAW * HEAD_SIZE)
    raw_copies = (
        raw_copy(k_ref.at[:, pl.ds(0, HEAD_SIZE)], raw_k.at[pl.ds(2 * rows, rows)], 0),
        raw_copy(v_ref.at[:, pl.ds(0, HEAD_SIZE)], raw_v.at[pl.ds(2 * rows, rows)], 1),
        raw_copy(q_ref.at[:, raw_columns], raw_q, 2),
        raw_copy(doc_ref, doc_last, 3),
    )
    doc_copy = pltpu.make_async_copy(doc_ref, doc_own, doc_sem)

    pairs = ((k_ref, k_buf), (v_ref, v_buf))
    doc_copy.start()
    for group in range(KEY_VALUE_HEADS):
        for which, (source, buf) in enumerate(pairs):
            own_copy(source, buf, group, which).start()
        q_copy(group).start()

    pl.semaphore_wait(barrier, 6)
    for copy in raw_copies:
        copy.start()
    for group in range(KEY_VALUE_HEADS):
        for which, (source, buf) in enumerate(pairs):
            for far in (1, 0):
                halo(source, buf, group, which, far).start()

    def fill_bias(docs):
        base = me * rows
        position = base + lax.broadcasted_iota(jnp.int32, (rows, rows), 0)
        column = lax.broadcasted_iota(jnp.int32, (rows, rows), 1)
        start = jnp.zeros((rows, rows), jnp.int32)
        end = jnp.zeros((1, 1), jnp.int32)
        for doc in range(docs.shape[1]):
            end = end + docs[0:1, doc:doc + 1]
            start = jnp.where(end <= position, jnp.maximum(start, end), start)
        for place in range(3):
            key = base + (place - 2) * rows + column
            allowed = (key >= start) & (key <= position)
            bias[:, place * rows:(place + 1) * rows] = jnp.where(allowed, 0.0, -jnp.inf)

    def attend(query, keys, values):
        scores = lax.dot_general(
            query, keys, (((1,), (1,)), ((), ())),
            preferred_element_type=jnp.float32,
        ) + bias[...]
        most = jnp.max(scores, axis=1, keepdims=True)
        weights = jnp.exp2((scores - most) * FACTOR)
        total = jnp.sum(weights, axis=1, keepdims=True)
        mixed = jnp.dot(
            weights.astype(jnp.bfloat16), values, preferred_element_type=jnp.float32
        )
        return (mixed / total).astype(jnp.bfloat16)

    doc_copy.wait()
    fill_bias(doc_own)

    for group in range(KEY_VALUE_HEADS):
        q_copy(group).wait()
        for which, (source, buf) in enumerate(pairs):
            own_copy(source, buf, group, which).wait()
            for far in (1, 0):
                halo(source, buf, group, which, far).wait_recv()

        @pl.loop(group * GROUP if group else RAW, (group + 1) * GROUP)
        def _(head):
            stage[:, columns(head)] = attend(
                q_buf[:, columns(head)], k_buf[group], v_buf[group]
            )
            out_copy(head).start()

        if group == 1:
            for copy in raw_copies:
                copy.wait_recv()
            for which, buf in enumerate((raw_k, raw_v)):
                for far in (1, 0):
                    relay(buf, which, far).start()

    fill_bias(doc_last)
    for which, buf in enumerate((raw_k, raw_v)):
        for far in (1, 0):
            relay(buf, which, far).wait_recv()

    @pl.loop(0, RAW)
    def _(head):
        out_ref[:, columns(head)] = attend(
            raw_q[:, columns(head)], raw_k[...], raw_v[...]
        )

    for copy in raw_copies:
        copy.wait_send()
    for which, buf in enumerate((raw_k, raw_v)):
        for far in (1, 0):
            relay(buf, which, far).wait_send()
    for group in range(KEY_VALUE_HEADS):
        for which, (source, buf) in enumerate(pairs):
            for far in (1, 0):
                halo(source, buf, group, which, far).wait_send()

    @pl.loop(RAW, QUERY_HEADS)
    def _(head):
        out_copy(head).wait()


def solution(mesh):
    n_seq, n_sec = mesh.shape["seq"], mesh.shape["section"]

    def local(query_projection, k_proj, value_projection, doc_lengths):
        rows, width = query_projection.shape[1:]
        hbm_spec = pl.BlockSpec(memory_space=pltpu.HBM)
        arrays = (query_projection[0], k_proj[0], value_projection[0], doc_lengths)
        operands = [pltpu.with_memory_space_constraint(x, pltpu.HBM) for x in arrays]
        result = pl.pallas_call(
            functools.partial(kernel, n_seq, n_sec),
            out_shape=jax.ShapeDtypeStruct((rows, width), jnp.bfloat16),
            in_specs=[hbm_spec] * 4,
            out_specs=pl.BlockSpec(memory_space=pltpu.VMEM),
            scratch_shapes=[
                pltpu.VMEM((rows, width), jnp.bfloat16),
                pltpu.VMEM((KEY_VALUE_HEADS, 3 * rows, HEAD_SIZE), jnp.bfloat16),
                pltpu.VMEM((KEY_VALUE_HEADS, 3 * rows, HEAD_SIZE), jnp.bfloat16),
                pltpu.VMEM((rows, 3 * rows), jnp.float32),
                pltpu.VMEM((rows, width), jnp.bfloat16),
                pltpu.VMEM(doc_lengths.shape, jnp.int32),
                pltpu.VMEM(doc_lengths.shape, jnp.int32),
                pltpu.VMEM((rows, RAW * HEAD_SIZE), jnp.bfloat16),
                pltpu.VMEM((3 * rows, HEAD_SIZE), jnp.bfloat16),
                pltpu.VMEM((3 * rows, HEAD_SIZE), jnp.bfloat16),
                pltpu.SemaphoreType.DMA((KEY_VALUE_HEADS,)),
                pltpu.SemaphoreType.DMA((KEY_VALUE_HEADS, 2)),
                pltpu.SemaphoreType.DMA((KEY_VALUE_HEADS, 2, 2)),
                pltpu.SemaphoreType.DMA((KEY_VALUE_HEADS, 2, 2)),
                pltpu.SemaphoreType.DMA((QUERY_HEADS,)),
                pltpu.SemaphoreType.DMA((QUERY_HEADS,)),
                pltpu.SemaphoreType.DMA,
                pltpu.SemaphoreType.DMA((4,)),
                pltpu.SemaphoreType.DMA((4,)),
                pltpu.SemaphoreType.DMA((2, 2)),
                pltpu.SemaphoreType.DMA((2, 2)),
            ],
            compiler_params=pltpu.CompilerParams(
                collective_id=0, has_side_effects=True, vmem_limit_bytes=24 * 2**20
            ),
        )(*operands)
        return result[None]

    in_specs = (
        P("section", "seq", None),
        P("section", "seq", None),
        P("section", "seq", None),
        P("section", None),
    )
    return jax.shard_map(
        local, mesh=mesh, in_specs=in_specs, out_specs=P("section", "seq", None),
        check_vma=False,
    )
```

```python
import functools
import math

import jax
import jax.numpy as jnp
from jax import lax
from jax.experimental import pallas as pl
from jax.experimental.pallas import tpu as pltpu
from jax.sharding import PartitionSpec as P

QUERY_HEADS = 32
KEY_VALUE_HEADS = 4
HEAD_SIZE = 128
GROUP = QUERY_HEADS // KEY_VALUE_HEADS
RAW = 5
MESH = pl.DeviceIdType.MESH
FACTOR = math.log2(math.e) / math.sqrt(HEAD_SIZE)


def kernel(
    n_seq, n_sec, q_ref, k_ref, v_ref, doc_ref, out_ref,
    q_buf, k_buf, v_buf, bias, stage, doc_own, doc_last, raw_q, raw_k, raw_v,
    q_sem, own_sem, halo_send, halo_recv, out_send, out_recv,
    doc_sem, raw_send, raw_recv, relay_send, relay_recv,
):
    rows = q_ref.shape[0]
    me = lax.axis_index("seq")
    sec = lax.axis_index("section")
    to_one = lax.rem(me + 1, n_seq)
    to_two = lax.rem(me + 2, n_seq)
    from_one = lax.rem(me + n_seq - 1, n_seq)
    from_two = lax.rem(me + n_seq - 2, n_seq)
    next_sec = lax.rem(sec + 1, n_sec)
    last_sec = lax.rem(sec + n_sec - 1, n_sec)

    barrier = pltpu.get_barrier_semaphore()
    for other in (from_one, from_two, to_one, to_two):
        pl.semaphore_signal(
            barrier, inc=1, device_id={"seq": other}, device_id_type=MESH
        )
    for other in (next_sec, last_sec):
        pl.semaphore_signal(
            barrier, inc=1, device_id={"section": other}, device_id_type=MESH
        )

    def columns(head, count=1):
        return pl.ds(pl.multiple_of(head * HEAD_SIZE, HEAD_SIZE), count * HEAD_SIZE)

    def own_copy(source, buf, group, which):
        return pltpu.make_async_copy(
            source.at[:, columns(group)],
            buf.at[group, pl.ds(2 * rows, rows)],
            own_sem.at[group, which],
        )

    def q_copy(group):
        return pltpu.make_async_copy(
            q_ref.at[:, columns(group * GROUP, GROUP)],
            q_buf.at[:, columns(group * GROUP, GROUP)],
            q_sem.at[group],
        )

    def halo(source, buf, group, which, far):
        return pltpu.make_async_remote_copy(
            src_ref=source.at[:, columns(group)],
            dst_ref=buf.at[group, pl.ds(0 if far else rows, rows)],
            send_sem=halo_send.at[group, which, far],
            recv_sem=halo_recv.at[group, which, far],
            device_id={"seq": to_two if far else to_one},
            device_id_type=MESH,
        )

    def out_copy(head):
        return pltpu.make_async_remote_copy(
            src_ref=stage.at[:, columns(head)],
            dst_ref=out_ref.at[:, columns(head)],
            send_sem=out_send.at[head],
            recv_sem=out_recv.at[head],
            device_id={"section": next_sec},
            device_id_type=MESH,
        )

    def raw_copy(source, buf, which):
        return pltpu.make_async_remote_copy(
            src_ref=source,
            dst_ref=buf,
            send_sem=raw_send.at[which],
            recv_sem=raw_recv.at[which],
            device_id={"section": next_sec},
            device_id_type=MESH,
        )

    def relay(buf, which, far):
        return pltpu.make_async_remote_copy(
            src_ref=buf.at[pl.ds(2 * rows, rows)],
            dst_ref=buf.at[pl.ds(0 if far else rows, rows)],
            send_sem=relay_send.at[which, far],
            recv_sem=relay_recv.at[which, far],
            device_id={"seq": to_two if far else to_one},
            device_id_type=MESH,
        )

    raw_columns = pl.ds(0, RAW * HEAD_SIZE)
    raw_copies = (
        raw_copy(k_ref.at[:, pl.ds(0, HEAD_SIZE)], raw_k.at[pl.ds(2 * rows, rows)], 0),
        raw_copy(v_ref.at[:, pl.ds(0, HEAD_SIZE)], raw_v.at[pl.ds(2 * rows, rows)], 1),
        raw_copy(q_ref.at[:, raw_columns], raw_q, 2),
        raw_copy(doc_ref, doc_last, 3),
    )
    doc_copy = pltpu.make_async_copy(doc_ref, doc_own, doc_sem)

    pairs = ((k_ref, k_buf), (v_ref, v_buf))
    doc_copy.start()
    for group in range(KEY_VALUE_HEADS):
        for which, (source, buf) in enumerate(pairs):
            own_copy(source, buf, group, which).start()
        q_copy(group).start()

    pl.semaphore_wait(barrier, 6)
    for copy in raw_copies:
        copy.start()
    for group in range(KEY_VALUE_HEADS):
        for which, (source, buf) in enumerate(pairs):
            for far in (1, 0):
                halo(source, buf, group, which, far).start()

    def fill_bias(docs):
        base = me * rows
        position = base + lax.broadcasted_iota(jnp.int32, (rows, rows), 0)
        column = lax.broadcasted_iota(jnp.int32, (rows, rows), 1)
        start = jnp.zeros((rows, rows), jnp.int32)
        end = jnp.zeros((1, 1), jnp.int32)
        for doc in range(docs.shape[1]):
            end = end + docs[0:1, doc:doc + 1]
            start = jnp.where(end <= position, jnp.maximum(start, end), start)
        for place in range(3):
            key = base + (place - 2) * rows + column
            allowed = (key >= start) & (key <= position)
            bias[:, place * rows:(place + 1) * rows] = jnp.where(allowed, 0.0, -jnp.inf)

    def attend(query, keys, values):
        scores = lax.dot_general(
            query, keys, (((1,), (1,)), ((), ())),
            preferred_element_type=jnp.float32,
        ) + bias[...]
        most = jnp.max(scores, axis=1, keepdims=True)
        weights = jnp.exp2((scores - most) * FACTOR)
        total = jnp.sum(weights, axis=1, keepdims=True)
        mixed = jnp.dot(
            weights.astype(jnp.bfloat16), values, preferred_element_type=jnp.float32
        )
        return (mixed / total).astype(jnp.bfloat16)

    doc_copy.wait()
    fill_bias(doc_own)

    for group in range(KEY_VALUE_HEADS):
        q_copy(group).wait()
        for which, (source, buf) in enumerate(pairs):
            own_copy(source, buf, group, which).wait()
            for far in (1, 0):
                halo(source, buf, group, which, far).wait_recv()

        @pl.loop(group * GROUP if group else RAW, (group + 1) * GROUP)
        def _(head):
            stage[:, columns(head)] = attend(
                q_buf[:, columns(head)], k_buf[group], v_buf[group]
            )

            @pl.when(head > RAW)
            def _():
                out_copy(head - 1).start()

        if group == 1:
            for copy in raw_copies:
                copy.wait_recv()
            for which, buf in enumerate((raw_k, raw_v)):
                for far in (1, 0):
                    relay(buf, which, far).start()

    fill_bias(doc_last)
    out_copy(QUERY_HEADS - 1).start()
    for which, buf in enumerate((raw_k, raw_v)):
        for far in (1, 0):
            relay(buf, which, far).wait_recv()

    @pl.loop(0, RAW)
    def _(head):
        out_ref[:, columns(head)] = attend(
            raw_q[:, columns(head)], raw_k[...], raw_v[...]
        )

    for copy in raw_copies:
        copy.wait_send()
    for which, buf in enumerate((raw_k, raw_v)):
        for far in (1, 0):
            relay(buf, which, far).wait_send()
    for group in range(KEY_VALUE_HEADS):
        for which, (source, buf) in enumerate(pairs):
            for far in (1, 0):
                halo(source, buf, group, which, far).wait_send()

    @pl.loop(RAW, QUERY_HEADS)
    def _(head):
        out_copy(head).wait()


def solution(mesh):
    n_seq, n_sec = mesh.shape["seq"], mesh.shape["section"]

    def local(query_projection, k_proj, value_projection, doc_lengths):
        rows, width = query_projection.shape[1:]
        hbm_spec = pl.BlockSpec(memory_space=pltpu.HBM)
        arrays = (query_projection[0], k_proj[0], value_projection[0], doc_lengths)
        operands = [pltpu.with_memory_space_constraint(x, pltpu.HBM) for x in arrays]
        result = pl.pallas_call(
            functools.partial(kernel, n_seq, n_sec),
            out_shape=jax.ShapeDtypeStruct((rows, width), jnp.bfloat16),
            in_specs=[hbm_spec] * 4,
            out_specs=pl.BlockSpec(memory_space=pltpu.VMEM),
            scratch_shapes=[
                pltpu.VMEM((rows, width), jnp.bfloat16),
                pltpu.VMEM((KEY_VALUE_HEADS, 3 * rows, HEAD_SIZE), jnp.bfloat16),
                pltpu.VMEM((KEY_VALUE_HEADS, 3 * rows, HEAD_SIZE), jnp.bfloat16),
                pltpu.VMEM((rows, 3 * rows), jnp.float32),
                pltpu.VMEM((rows, width), jnp.bfloat16),
                pltpu.VMEM(doc_lengths.shape, jnp.int32),
                pltpu.VMEM(doc_lengths.shape, jnp.int32),
                pltpu.VMEM((rows, RAW * HEAD_SIZE), jnp.bfloat16),
                pltpu.VMEM((3 * rows, HEAD_SIZE), jnp.bfloat16),
                pltpu.VMEM((3 * rows, HEAD_SIZE), jnp.bfloat16),
                pltpu.SemaphoreType.DMA((KEY_VALUE_HEADS,)),
                pltpu.SemaphoreType.DMA((KEY_VALUE_HEADS, 2)),
                pltpu.SemaphoreType.DMA((KEY_VALUE_HEADS, 2, 2)),
                pltpu.SemaphoreType.DMA((KEY_VALUE_HEADS, 2, 2)),
                pltpu.SemaphoreType.DMA((QUERY_HEADS,)),
                pltpu.SemaphoreType.DMA((QUERY_HEADS,)),
                pltpu.SemaphoreType.DMA,
                pltpu.SemaphoreType.DMA((4,)),
                pltpu.SemaphoreType.DMA((4,)),
                pltpu.SemaphoreType.DMA((2, 2)),
                pltpu.SemaphoreType.DMA((2, 2)),
            ],
            compiler_params=pltpu.CompilerParams(
                collective_id=0, has_side_effects=True, vmem_limit_bytes=24 * 2**20
            ),
        )(*operands)
        return result[None]

    in_specs = (
        P("section", "seq", None),
        P("section", "seq", None),
        P("section", "seq", None),
        P("section", None),
    )
    return jax.shard_map(
        local, mesh=mesh, in_specs=in_specs, out_specs=P("section", "seq", None),
        check_vma=False,
    )
```

```python
import functools
import math

import jax
import jax.numpy as jnp
from jax import lax
from jax.experimental import pallas as pl
from jax.experimental.pallas import tpu as pltpu
from jax.sharding import PartitionSpec as P

QUERY_HEADS = 32
KEY_VALUE_HEADS = 4
HEAD_SIZE = 128
GROUP = QUERY_HEADS // KEY_VALUE_HEADS
RAW = 5
RAW_ODD = 3
MESH = pl.DeviceIdType.MESH
FACTOR = math.log2(math.e) / math.sqrt(HEAD_SIZE)


def kernel(
    n_seq, n_sec, q_ref, k_ref, v_ref, doc_ref, out_ref,
    q_buf, k_buf, v_buf, bias, stage, doc_own, doc_last, raw_q, raw_k, raw_v,
    q_sem, own_sem, halo_send, halo_recv, out_send, out_recv,
    doc_sem, raw_send, raw_recv, relay_send, relay_recv,
):
    rows = q_ref.shape[0]
    me = lax.axis_index("seq")
    sec = lax.axis_index("section")
    to_one = lax.rem(me + 1, n_seq)
    to_two = lax.rem(me + 2, n_seq)
    from_one = lax.rem(me + n_seq - 1, n_seq)
    from_two = lax.rem(me + n_seq - 2, n_seq)
    next_sec = lax.rem(sec + 1, n_sec)
    last_sec = lax.rem(sec + n_sec - 1, n_sec)

    barrier = pltpu.get_barrier_semaphore()
    for other in (from_one, from_two, to_one, to_two):
        pl.semaphore_signal(
            barrier, inc=1, device_id={"seq": other}, device_id_type=MESH
        )
    for other in (next_sec, last_sec):
        pl.semaphore_signal(
            barrier, inc=1, device_id={"section": other}, device_id_type=MESH
        )

    def columns(head, count=1):
        return pl.ds(pl.multiple_of(head * HEAD_SIZE, HEAD_SIZE), count * HEAD_SIZE)

    def own_copy(source, buf, group, which):
        return pltpu.make_async_copy(
            source.at[:, columns(group)],
            buf.at[group, pl.ds(2 * rows, rows)],
            own_sem.at[group, which],
        )

    def q_copy(group):
        return pltpu.make_async_copy(
            q_ref.at[:, columns(group * GROUP, GROUP)],
            q_buf.at[:, columns(group * GROUP, GROUP)],
            q_sem.at[group],
        )

    def halo(source, buf, group, which, far):
        return pltpu.make_async_remote_copy(
            src_ref=source.at[:, columns(group)],
            dst_ref=buf.at[group, pl.ds(0 if far else rows, rows)],
            send_sem=halo_send.at[group, which, far],
            recv_sem=halo_recv.at[group, which, far],
            device_id={"seq": to_two if far else to_one},
            device_id_type=MESH,
        )

    def out_copy(head):
        return pltpu.make_async_remote_copy(
            src_ref=stage.at[:, columns(head)],
            dst_ref=out_ref.at[:, columns(head)],
            send_sem=out_send.at[head],
            recv_sem=out_recv.at[head],
            device_id={"section": next_sec},
            device_id_type=MESH,
        )

    def raw_copy(source, buf, which):
        return pltpu.make_async_remote_copy(
            src_ref=source,
            dst_ref=buf,
            send_sem=raw_send.at[which],
            recv_sem=raw_recv.at[which],
            device_id={"section": next_sec},
            device_id_type=MESH,
        )

    def relay(buf, which, far):
        return pltpu.make_async_remote_copy(
            src_ref=buf.at[pl.ds(2 * rows, rows)],
            dst_ref=buf.at[pl.ds(0 if far else rows, rows)],
            send_sem=relay_send.at[which, far],
            recv_sem=relay_recv.at[which, far],
            device_id={"seq": to_two if far else to_one},
            device_id_type=MESH,
        )

    raw_columns = pl.ds(0, RAW_ODD * HEAD_SIZE)
    more_columns = pl.ds(RAW_ODD * HEAD_SIZE, (RAW - RAW_ODD) * HEAD_SIZE)
    even = lax.rem(me, 2) == 0
    first = RAW - (RAW - RAW_ODD) * lax.rem(me, 2)
    raw_copies = (
        raw_copy(k_ref.at[:, pl.ds(0, HEAD_SIZE)], raw_k.at[pl.ds(2 * rows, rows)], 0),
        raw_copy(v_ref.at[:, pl.ds(0, HEAD_SIZE)], raw_v.at[pl.ds(2 * rows, rows)], 1),
        raw_copy(q_ref.at[:, raw_columns], raw_q.at[:, raw_columns], 2),
        raw_copy(doc_ref, doc_last, 3),
    )
    more_copy = raw_copy(q_ref.at[:, more_columns], raw_q.at[:, more_columns], 4)
    doc_copy = pltpu.make_async_copy(doc_ref, doc_own, doc_sem)

    pairs = ((k_ref, k_buf), (v_ref, v_buf))
    doc_copy.start()
    for group in range(KEY_VALUE_HEADS):
        for which, (source, buf) in enumerate(pairs):
            own_copy(source, buf, group, which).start()
        q_copy(group).start()

    pl.semaphore_wait(barrier, 6)
    for copy in raw_copies:
        copy.start()

    @pl.when(even)
    def _():
        more_copy.start()

    for group in range(KEY_VALUE_HEADS):
        for which, (source, buf) in enumerate(pairs):
            for far in (1, 0):
                halo(source, buf, group, which, far).start()

    def fill_bias(docs):
        base = me * rows
        position = base + lax.broadcasted_iota(jnp.int32, (rows, rows), 0)
        column = lax.broadcasted_iota(jnp.int32, (rows, rows), 1)
        start = jnp.zeros((rows, rows), jnp.int32)
        end = jnp.zeros((1, 1), jnp.int32)
        for doc in range(docs.shape[1]):
            end = end + docs[0:1, doc:doc + 1]
            start = jnp.where(end <= position, jnp.maximum(start, end), start)
        for place in range(3):
            key = base + (place - 2) * rows + column
            allowed = (key >= start) & (key <= position)
            bias[:, place * rows:(place + 1) * rows] = jnp.where(allowed, 0.0, -jnp.inf)

    def attend(query, keys, values):
        scores = lax.dot_general(
            query, keys, (((1,), (1,)), ((), ())),
            preferred_element_type=jnp.float32,
        ) + bias[...]
        most = jnp.max(scores, axis=1, keepdims=True)
        weights = jnp.exp2((scores - most) * FACTOR)
        total = jnp.sum(weights, axis=1, keepdims=True)
        mixed = jnp.dot(
            weights.astype(jnp.bfloat16), values, preferred_element_type=jnp.float32
        )
        return (mixed / total).astype(jnp.bfloat16)

    doc_copy.wait()
    fill_bias(doc_own)

    for group in range(KEY_VALUE_HEADS):
        q_copy(group).wait()
        for which, (source, buf) in enumerate(pairs):
            own_copy(source, buf, group, which).wait()
            for far in (1, 0):
                halo(source, buf, group, which, far).wait_recv()

        @pl.loop(group * GROUP if group else first, (group + 1) * GROUP)
        def _(head):
            stage[:, columns(head)] = attend(
                q_buf[:, columns(head)], k_buf[group], v_buf[group]
            )
            out_copy(head).start()

        if group == 1:
            for copy in raw_copies:
                copy.wait_recv()

            @pl.when(even)
            def _():
                more_copy.wait_recv()

            for which, buf in enumerate((raw_k, raw_v)):
                for far in (1, 0):
                    relay(buf, which, far).start()

    fill_bias(doc_last)
    for which, buf in enumerate((raw_k, raw_v)):
        for far in (1, 0):
            relay(buf, which, far).wait_recv()

    @pl.loop(0, first)
    def _(head):
        out_ref[:, columns(head)] = attend(
            raw_q[:, columns(head)], raw_k[...], raw_v[...]
        )

    for copy in raw_copies:
        copy.wait_send()

    @pl.when(even)
    def _():
        more_copy.wait_send()

    for which, buf in enumerate((raw_k, raw_v)):
        for far in (1, 0):
            relay(buf, which, far).wait_send()
    for group in range(KEY_VALUE_HEADS):
        for which, (source, buf) in enumerate(pairs):
            for far in (1, 0):
                halo(source, buf, group, which, far).wait_send()

    @pl.loop(first, QUERY_HEADS)
    def _(head):
        out_copy(head).wait()


def solution(mesh):
    n_seq, n_sec = mesh.shape["seq"], mesh.shape["section"]

    def local(query_projection, k_proj, value_projection, doc_lengths):
        rows, width = query_projection.shape[1:]
        hbm_spec = pl.BlockSpec(memory_space=pltpu.HBM)
        arrays = (query_projection[0], k_proj[0], value_projection[0], doc_lengths)
        operands = [pltpu.with_memory_space_constraint(x, pltpu.HBM) for x in arrays]
        result = pl.pallas_call(
            functools.partial(kernel, n_seq, n_sec),
            out_shape=jax.ShapeDtypeStruct((rows, width), jnp.bfloat16),
            in_specs=[hbm_spec] * 4,
            out_specs=pl.BlockSpec(memory_space=pltpu.VMEM),
            scratch_shapes=[
                pltpu.VMEM((rows, width), jnp.bfloat16),
                pltpu.VMEM((KEY_VALUE_HEADS, 3 * rows, HEAD_SIZE), jnp.bfloat16),
                pltpu.VMEM((KEY_VALUE_HEADS, 3 * rows, HEAD_SIZE), jnp.bfloat16),
                pltpu.VMEM((rows, 3 * rows), jnp.float32),
                pltpu.VMEM((rows, width), jnp.bfloat16),
                pltpu.VMEM(doc_lengths.shape, jnp.int32),
                pltpu.VMEM(doc_lengths.shape, jnp.int32),
                pltpu.VMEM((rows, RAW * HEAD_SIZE), jnp.bfloat16),
                pltpu.VMEM((3 * rows, HEAD_SIZE), jnp.bfloat16),
                pltpu.VMEM((3 * rows, HEAD_SIZE), jnp.bfloat16),
                pltpu.SemaphoreType.DMA((KEY_VALUE_HEADS,)),
                pltpu.SemaphoreType.DMA((KEY_VALUE_HEADS, 2)),
                pltpu.SemaphoreType.DMA((KEY_VALUE_HEADS, 2, 2)),
                pltpu.SemaphoreType.DMA((KEY_VALUE_HEADS, 2, 2)),
                pltpu.SemaphoreType.DMA((QUERY_HEADS,)),
                pltpu.SemaphoreType.DMA((QUERY_HEADS,)),
                pltpu.SemaphoreType.DMA,
                pltpu.SemaphoreType.DMA((5,)),
                pltpu.SemaphoreType.DMA((5,)),
                pltpu.SemaphoreType.DMA((2, 2)),
                pltpu.SemaphoreType.DMA((2, 2)),
            ],
            compiler_params=pltpu.CompilerParams(
                collective_id=0, has_side_effects=True, vmem_limit_bytes=24 * 2**20
            ),
        )(*operands)
        return result[None]

    in_specs = (
        P("section", "seq", None),
        P("section", "seq", None),
        P("section", "seq", None),
        P("section", None),
    )
    return jax.shard_map(
        local, mesh=mesh, in_specs=in_specs, out_specs=P("section", "seq", None),
        check_vma=False,
    )
```
